32 devices in a mesh: rep: 4 (over y, x), tp: 8 (over z, core).
Axes of the slice: x: 2, y: 2, z: 4, core: 2. Of those that a mesh axis runs over, the one named last changes fastest.
Arguments:
- hidden_states: bfloat16 [3, 32, 16384], P(None, 'rep'), may hold values from -6 to 6
- query_mantissa: bfloat16 [128, 128, 8192], P('rep', None, 'tp'), may hold values from -6 to 6
- query_exponent: int32 [128, 8192], P('rep', 'tp'), may hold values from -10 to -6
- keyval_mantissa: bfloat16 [128, 128, 1024], P('rep', None, 'tp'), may hold values from -6 to 6
- keyval_exponent: int32 [128, 1024], P('rep', 'tp'), may hold values from -10 to -6
- owner_block: int32 [4], replicated, may hold values from 0 to 3, each once
- cached_kv: bfloat16 [32, 256, 1024], P(('rep', 'tp')), may hold values from -2048 to 2048
- cache_length: int32 [32], P(('rep', 'tp')), may hold values from 2 to 256, as said below
Outputs:
- attended: bfloat16 [3, 32, 8192], P(None, 'rep', 'tp')
The draws below stay inside these ranges and needn't reach their ends.
Inputs may be any that keep to these rules, and one draw needn't show every extreme that they name: `owner_block`: each rep index appears once. `cache_length`: some row has exactly 256 filled slots.
All inputs are finite; a program needn't handle non-finite values.
Results may differ from the reference program's by a relative error of at most 0.017.
The reference program's roundings to bfloat16 on the way (of `query_weight`, `keyval_weight`, `queries`, `keyvals`, `query_rot` and `weights`) count: a program that leaves them out, or rounds other values in their place, can miss the bound.
Values may be sent and summed in bfloat16 or wider, within the bound.
No kernel may reach another device: no remote copies, remote signals or barrier semaphores. Data moves between devices by JAX's collectives and lax.ppermute only.
A program may use at most 64 MiB of HBM per device.

```python
import math
import jax
import jax.numpy as jnp
from jax import lax

D = 16384
QH = 64
KVH = 4
HD = 128
BLK = 128
STEPS = 3
CACHE = 256
ROWS = 32
NBLK = 128
QCOLS = 8192
KVCOLS = 1024
N_REP = 4


def draw_cached_kv(key, part):
    key_first = jax.random.fold_in(jax.random.fold_in(key, 11), 0)
    values = jax.random.truncated_normal(key_first, -6.0, 6.0, (ROWS, CACHE, 2 * KVH * HD), jnp.float32)
    return values.astype(jnp.bfloat16)


def draw_cache_length(key, part):
    key_first, key_second = jax.random.split(jax.random.fold_in(key, 23), 2)
    values = jax.random.randint(key_first, (ROWS,), 2, CACHE + 1, jnp.int32)
    chosen = jax.random.randint(key_second, (), 0, ROWS, jnp.int32)
    return jnp.where(jnp.arange(ROWS, dtype=jnp.int32) == chosen, CACHE, values).astype(jnp.int32)


def with_ends(array, key, least, largest):
    index_at = [jax.random.randint(jax.random.fold_in(key, axis), (), 0, length) for axis, length in enumerate(array.shape)]
    longest = array.shape.index(max(array.shape))
    next_to = index_at[:longest] + [(index_at[longest] + 1) % array.shape[longest]] + index_at[longest + 1:]
    return array.at[tuple(index_at)].set(least).at[tuple(next_to)].set(largest)


def steps_of(stream_key, shape, cuts, low, top_value):
    factor_of, own = 1.0, jax.random.fold_in(stream_key, 6)
    for dim, shards_of in cuts:
        steps = jnp.exp(jax.random.uniform(jax.random.fold_in(own, dim), (shards_of,), jnp.float32, low / len(cuts), top_value / len(cuts)))
        factor_of = factor_of * jnp.repeat(steps, shape[dim] // shards_of).reshape([-1 if axis == dim else 1 for axis in range(len(shape))])
    return factor_of


def scatter_about(own_key, dims, scale, limit, pieces=(), kind=jnp.bfloat16):
    entries = scale * jax.random.normal(own_key, dims, jnp.float32)
    if pieces:
        entries = entries * steps_of(own_key, dims, pieces, -0.22, 0.18)
    return jnp.clip(entries, -limit, limit).astype(kind)


def setup_inputs(seed: int = 0) -> dict:
    splits = jax.random.split(jax.random.key(seed), 9)
    hidden_states = scatter_about(splits[0], (STEPS, ROWS, D), 1.0, 6.0, ((1, 4),))
    query_mantissa = scatter_about(splits[1], (NBLK, BLK, QCOLS), 1.0, 6.0, ((0, 4), (2, 8)))
    query_exponent = with_ends(jax.random.randint(splits[2], (NBLK, QCOLS), -10, -5), jax.random.fold_in(splits[2], 1), -10, (-5) - 1).astype(jnp.int32)
    keyval_mantissa = scatter_about(splits[3], (NBLK, BLK, KVCOLS), 1.0, 6.0, ((0, 4), (2, 8)))
    keyval_exponent = with_ends(jax.random.randint(splits[4], (NBLK, KVCOLS), -10, -5), jax.random.fold_in(splits[4], 1), -10, (-5) - 1).astype(jnp.int32)
    owner_block = jax.random.permutation(splits[5], N_REP).astype(jnp.int32)
    cached_kv = draw_cached_kv(jax.random.fold_in(splits[8], 71), 0)
    cache_length = draw_cache_length(jax.random.fold_in(splits[8], 71), 0)
    return {"hidden_states": hidden_states, "query_mantissa": query_mantissa, "query_exponent": query_exponent, "keyval_mantissa": keyval_mantissa, "keyval_exponent": keyval_exponent, "owner_block": owner_block, "cached_kv": cached_kv, "cache_length": cache_length}


def dequantize(mantissa, exponent):
    factor = jnp.exp2(exponent.astype(jnp.float32))
    return (mantissa.astype(jnp.float32) * factor[:, None, :]).astype(jnp.bfloat16)

def rotate(vectors, position):
    half_size = vectors.shape[-1] // 2
    frequency = jnp.exp(jnp.arange(half_size, dtype=jnp.float32) * (-2.0 * math.log(500000.0) / vectors.shape[-1]))
    angles = position * frequency
    cosine = jnp.cos(angles)
    sine = jnp.sin(angles)
    leading = vectors[..., :half_size]
    trailing = vectors[..., half_size:]
    return jnp.concatenate([leading * cosine - trailing * sine, trailing * cosine + leading * sine], axis=-1)

def attend_row(query_rot, new_keys, new_values, cache_row, row_length):
    old_keys = cache_row[:, :KVH * HD].reshape(CACHE, KVH, HD).astype(jnp.float32)
    old_values = cache_row[:, KVH * HD:].reshape(CACHE, KVH, HD).astype(jnp.float32)
    grouped = query_rot.reshape(STEPS, KVH, QH // KVH, HD).astype(jnp.float32)
    score_scale = 1.0 / math.sqrt(HD)
    old_scores = jnp.einsum('tgjd,cgd->tgjc', grouped, old_keys) * score_scale
    new_scores = jnp.einsum('tgjd,sgd->tgjs', grouped, new_keys.astype(jnp.float32)) * score_scale
    old_valid = jnp.arange(CACHE, dtype=jnp.int32) < row_length
    new_valid = jnp.arange(STEPS, dtype=jnp.int32)[None, :] <= jnp.arange(STEPS, dtype=jnp.int32)[:, None]
    old_scores = jnp.where(old_valid[None, None, None, :], old_scores, -1e+30)
    new_scores = jnp.where(new_valid[:, None, None, :], new_scores, -1e+30)
    highest = jnp.maximum(lax.optimization_barrier(jnp.max(old_scores, axis=-1)), lax.optimization_barrier(jnp.max(new_scores, axis=-1)))[..., None]
    old_exp = jnp.exp(old_scores - highest)
    new_exp = jnp.exp(new_scores - highest)
    denominator = lax.optimization_barrier(jnp.sum(old_exp, axis=-1, keepdims=True)) + lax.optimization_barrier(jnp.sum(new_exp, axis=-1, keepdims=True))
    old_weights = lax.optimization_barrier((old_exp / denominator).astype(jnp.bfloat16)).astype(jnp.float32)
    new_weights = lax.optimization_barrier((new_exp / denominator).astype(jnp.bfloat16)).astype(jnp.float32)
    mixed = jnp.einsum('tgjc,cgd->tgjd', old_weights, old_values)
    mixed = mixed + jnp.einsum('tgjs,sgd->tgjd', new_weights, new_values.astype(jnp.float32))
    return mixed.astype(jnp.bfloat16).reshape(STEPS, QH * HD)

def reference(hidden_states, query_mantissa, query_exponent, keyval_mantissa, keyval_exponent, owner_block, cached_kv, cache_length):
    region = NBLK // N_REP
    stored = jnp.arange(NBLK, dtype=jnp.int32)
    target = (owner_block[stored // region] * region + stored % region).astype(jnp.int32)

    def unpack(mantissa, exponent):
        weights = dequantize(mantissa, exponent)
        placed = jnp.zeros_like(weights).at[target].set(weights)
        return placed.reshape(D, weights.shape[2])
    query_weight = unpack(query_mantissa, query_exponent)
    keyval_weight = unpack(keyval_mantissa, keyval_exponent)
    flat = hidden_states.reshape(STEPS * ROWS, D)
    queries = jnp.dot(flat, query_weight, preferred_element_type=jnp.float32).astype(jnp.bfloat16)
    queries = queries.reshape(STEPS, ROWS, QH, HD)
    keyvals = jnp.dot(flat, keyval_weight, preferred_element_type=jnp.float32).astype(jnp.bfloat16)
    keyvals = keyvals.reshape(STEPS, ROWS, 2, KVH, HD)
    positions = cache_length.astype(jnp.float32)[None, :] + jnp.arange(STEPS, dtype=jnp.float32)[:, None]
    query_rot = rotate(queries.astype(jnp.float32), positions[:, :, None, None]).astype(jnp.bfloat16)
    key_rot = rotate(keyvals[:, :, 0].astype(jnp.float32), positions[:, :, None, None]).astype(jnp.bfloat16)
    new_values = keyvals[:, :, 1]

    def one_row(packed):
        return attend_row(packed[0], packed[1], packed[2], packed[3], packed[4])
    attended = lax.map(one_row, (jnp.swapaxes(query_rot, 0, 1), jnp.swapaxes(key_rot, 0, 1), jnp.swapaxes(new_values, 0, 1), cached_kv, cache_length))
    return jnp.swapaxes(attended, 0, 1)
```

```python
import functools
import math

import jax
import jax.numpy as jnp
from jax import lax
from jax.experimental import pallas as pl
from jax.experimental.pallas import tpu as pltpu
from jax.sharding import PartitionSpec as P

QH = 64
KVH = 4
HD = 128
ROPE_BASE = 500000.0


def dequantize(mantissa, exponent):
    factor = jnp.exp2(exponent.astype(jnp.float32))
    return (mantissa.astype(jnp.float32) * factor[:, None, :]).astype(jnp.bfloat16)


def rotate(vectors, position):
    half_size = vectors.shape[-1] // 2
    frequency = jnp.exp(
        jnp.arange(half_size, dtype=jnp.float32) * (-2.0 * math.log(ROPE_BASE) / vectors.shape[-1])
    )
    angles = position * frequency
    cosine = jnp.cos(angles)
    sine = jnp.sin(angles)
    leading = vectors[..., :half_size]
    trailing = vectors[..., half_size:]
    return jnp.concatenate(
        [leading * cosine - trailing * sine, trailing * cosine + leading * sine], axis=-1
    )


def per_device_general(
    hidden_states,
    query_mantissa,
    query_exponent,
    keyval_mantissa,
    keyval_exponent,
    owner_block,
    cached_kv,
    cache_length,
):
    step_count, group_rows, model_width = hidden_states.shape
    region, block_size, query_cols = query_mantissa.shape
    keyval_cols = keyval_mantissa.shape[2]
    replicas = lax.axis_size("rep")
    flat_rows = step_count * group_rows
    flat = hidden_states.reshape(flat_rows, model_width)
    regions = flat.reshape(flat_rows, replicas, region * block_size)
    outgoing = jnp.take(regions, owner_block, axis=1)
    incoming = lax.all_to_all(outgoing, "rep", split_axis=1, concat_axis=0, tiled=True)
    incoming = incoming.reshape(replicas * flat_rows, region, block_size)
    joined = jnp.concatenate(
        [dequantize(query_mantissa, query_exponent), dequantize(keyval_mantissa, keyval_exponent)],
        axis=2,
    )
    both_sums = lax.psum_scatter(
        jnp.einsum("rbk,bkc->rc", incoming, joined, preferred_element_type=jnp.float32),
        "rep",
        scatter_dimension=0,
        tiled=True,
    )
    query_sum = both_sums[:, :query_cols]
    keyval_sum = both_sums[:, query_cols:]
    query_flat = query_sum.astype(jnp.bfloat16).reshape(step_count, group_rows, query_cols)
    keyval_flat = keyval_sum.astype(jnp.bfloat16).reshape(step_count, group_rows, keyval_cols)
    query_local, keyval_local = (
        lax.all_to_all(query_flat, "tp", split_axis=1, concat_axis=2, tiled=True),
        lax.all_to_all(keyval_flat, "tp", split_axis=1, concat_axis=2, tiled=True),
    )
    local_rows = cache_length.shape[0]
    cache_size = cached_kv.shape[1]
    positions = (
        cache_length.astype(jnp.float32)[None, :]
        + jnp.arange(step_count, dtype=jnp.float32)[:, None]
    )
    query_rot = rotate(
        query_local.reshape(step_count, local_rows, QH, HD).astype(jnp.float32),
        positions[:, :, None, None],
    ).astype(jnp.bfloat16)
    keyval_heads = keyval_local.reshape(step_count, local_rows, 2, KVH, HD)
    key_rot = rotate(keyval_heads[:, :, 0].astype(jnp.float32), positions[:, :, None, None]).astype(
        jnp.bfloat16
    )
    new_values = keyval_heads[:, :, 1]
    old_keys = cached_kv[:, :, : KVH * HD].reshape(local_rows, cache_size, KVH, HD)
    old_values = cached_kv[:, :, KVH * HD :].reshape(local_rows, cache_size, KVH, HD)
    grouped = query_rot.reshape(step_count, local_rows, KVH, QH // KVH, HD)
    score_scale = 1.0 / math.sqrt(HD)
    old_scores = (
        jnp.einsum("trgjd,rcgd->trgjc", grouped, old_keys, preferred_element_type=jnp.float32)
        * score_scale
    )
    new_scores = (
        jnp.einsum("trgjd,srgd->trgjs", grouped, key_rot, preferred_element_type=jnp.float32)
        * score_scale
    )
    old_valid = jnp.arange(cache_size, dtype=jnp.int32)[None, :] < cache_length[:, None]
    new_valid = (
        jnp.arange(step_count, dtype=jnp.int32)[None, :]
        <= jnp.arange(step_count, dtype=jnp.int32)[:, None]
    )
    old_scores = jnp.where(old_valid[None, :, None, None, :], old_scores, -1e30)
    new_scores = jnp.where(new_valid[:, None, None, None, :], new_scores, -1e30)
    highest = jnp.maximum(jnp.max(old_scores, axis=-1), jnp.max(new_scores, axis=-1))[..., None]
    old_exp = jnp.exp(old_scores - highest)
    new_exp = jnp.exp(new_scores - highest)
    denominator = jnp.sum(old_exp, axis=-1, keepdims=True) + jnp.sum(
        new_exp, axis=-1, keepdims=True
    )
    old_weights = (old_exp / denominator).astype(jnp.bfloat16)
    new_weights = (new_exp / denominator).astype(jnp.bfloat16)
    mixed = jnp.einsum(
        "trgjc,rcgd->trgjd", old_weights, old_values, preferred_element_type=jnp.float32
    )
    mixed = mixed + jnp.einsum(
        "trgjs,srgd->trgjd", new_weights, new_values, preferred_element_type=jnp.float32
    )
    outputs = mixed.astype(jnp.bfloat16).reshape(step_count, local_rows, QH * HD)
    return lax.all_to_all(outputs, "tp", split_axis=2, concat_axis=1, tiled=True)


WIRE = jnp.float32
CHUNK = 4
PAD = 16
DIGIT = 128


def project_kernel(replicas, *refs):
    slabs = refs[:replicas]
    qm_ref, qe_ref, kvm_ref, kve_ref = refs[replicas : replicas + 4]
    outs = refs[replicas + 4 : 2 * replicas + 4]
    lhs_ref, acc_ref, qf_ref, kvf_ref = refs[2 * replicas + 4 :]
    step = pl.program_id(0)
    rows = slabs[0].shape[0]
    chunk, block_size, query_cols = qm_ref.shape

    @pl.when(step == 0)
    def _():
        for k in range(replicas):
            lhs_ref[k * rows : (k + 1) * rows, :] = slabs[k][...]
        qf_ref[...] = jnp.exp2(qe_ref[...].astype(jnp.float32))
        kvf_ref[...] = jnp.exp2(kve_ref[...].astype(jnp.float32))
        acc_ref[...] = jnp.zeros_like(acc_ref)

    depth = chunk * block_size
    lhs = lhs_ref[:, pl.ds(pl.multiple_of(step * depth, depth), depth)]

    def product(m_ref, f_ref):
        pieces = []
        for b in range(chunk):
            factor = f_ref[pl.ds(step * chunk + b, 1), :].astype(jnp.bfloat16)
            pieces.append(m_ref[b] * factor)
        weight = jnp.concatenate(pieces, axis=0)
        return jnp.dot(lhs, weight, preferred_element_type=jnp.float32)

    acc_ref[:, :query_cols] += product(qm_ref, qf_ref)
    acc_ref[:, query_cols:] += product(kvm_ref, kvf_ref)

    @pl.when(step == pl.num_programs(0) - 1)
    def _():
        for k in range(replicas):
            outs[k][...] = acc_ref[k * rows : (k + 1) * rows, :].astype(outs[k].dtype)


def project(slabs, query_mantissa, query_exponent, keyval_mantissa, keyval_exponent):
    replicas = len(slabs)
    rows, depth = slabs[0].shape
    region, block_size, query_cols = query_mantissa.shape
    keyval_cols = keyval_mantissa.shape[2]
    cols = query_cols + keyval_cols
    whole = lambda *shape: pl.BlockSpec(shape, lambda s: (0,) * len(shape))
    return pl.pallas_call(
        functools.partial(project_kernel, replicas),
        grid=(region // CHUNK,),
        in_specs=[whole(rows, depth)] * replicas
        + [
            pl.BlockSpec((CHUNK, block_size, query_cols), lambda s: (s, 0, 0)),
            whole(region, query_cols),
            pl.BlockSpec((CHUNK, block_size, keyval_cols), lambda s: (s, 0, 0)),
            whole(region, keyval_cols),
        ],
        out_specs=[whole(rows, cols)] * replicas,
        out_shape=[
            jax.ShapeDtypeStruct((rows, cols), jnp.float32 if k == 0 else WIRE)
            for k in range(replicas)
        ],
        scratch_shapes=[
            pltpu.VMEM((replicas * rows, depth), jnp.bfloat16),
            pltpu.VMEM((replicas * rows, cols), jnp.float32),
            pltpu.VMEM((region, query_cols), jnp.float32),
            pltpu.VMEM((region, keyval_cols), jnp.float32),
        ],
        compiler_params=pltpu.CompilerParams(vmem_limit_bytes=24 * 2**20),
        name="project",
    )(*slabs, query_mantissa, query_exponent, keyval_mantissa, keyval_exponent)


def row_length(tail):
    tail = tail.astype(jnp.float32)
    return tail[0:1, 0:1] * DIGIT + tail[0:1, 1:2]


def tables_kernel(slots, slot_ref, *refs):
    tails = refs[:slots]
    cos_ref, sin_ref = refs[slots:]
    steps, group_rows, width = cos_ref.shape
    half = width // 2
    row = lax.broadcasted_iota(jnp.int32, (group_rows, width), 0)
    lane = lax.broadcasted_iota(jnp.int32, (group_rows, width), 1)
    length = jnp.zeros((group_rows, width), jnp.float32)
    for i in range(slots):
        length = jnp.where(row == slot_ref[i], row_length(tails[i][...]), length)
    index = jnp.where(lane < half, lane, lane - half).astype(jnp.float32)
    frequency = jnp.exp(index * (-2.0 * math.log(ROPE_BASE) / width))
    for t in range(steps):
        angles = (length + float(t)) * frequency
        cos_ref[t] = jnp.cos(angles)
        sine = jnp.sin(angles)
        sin_ref[t] = jnp.where(lane < half, -sine, sine)


def tables(slot_rows, slabs, steps, group_rows):
    slots = len(slabs)
    size = slabs[0].shape[0] // PAD - 1
    shape = (steps, group_rows, HD)
    whole = pl.BlockSpec(shape, lambda i: (0, 0, 0))
    return pl.pallas_call(
        functools.partial(tables_kernel, slots),
        grid=(1,),
        in_specs=[pl.BlockSpec(memory_space=pltpu.SMEM)]
        + [pl.BlockSpec((PAD, 2 * HD), lambda i: (size, 0))] * slots,
        out_specs=[whole, whole],
        out_shape=[jax.ShapeDtypeStruct(shape, jnp.float32)] * 2,
        name="tables",
    )(slot_rows, *slabs)


def attend_kernel(parts, slots, slot_ref, *refs):
    sums = refs[:parts]
    kn_ref, vn_ref, cos_ref, sin_ref = refs[parts : parts + 4]
    slabs = refs[parts + 4 : parts + 4 + slots]
    out_ref, q_scr, k_scr, v_scr, o_scr = refs[parts + 4 + slots :]
    steps, group_rows, query_cols = out_ref.shape
    heads = query_cols // HD
    half = HD // 2
    fresh = k_scr.shape[1]
    count = steps * heads
    cache_size = slabs[0].shape[0] - PAD

    def rotated(x, t):
        return x * cos_ref[t] + pltpu.roll(x, half, 1) * sin_ref[t]

    def rounded(x):
        return x.astype(jnp.bfloat16).astype(jnp.float32)

    for t in range(steps):
        rows = slice(t * group_rows, (t + 1) * group_rows)
        by_head = []
        for h in range(heads):
            cols = slice(h * HD, (h + 1) * HD)
            x = sums[0][rows, cols]
            for part in sums[1:]:
                x = x + part[rows, cols].astype(jnp.float32)
            by_head.append(rotated(rounded(x), t))
        turned = jnp.swapaxes(jnp.stack(by_head, axis=0), 0, 1)
        q_scr[:, t * heads : (t + 1) * heads, :] = turned.astype(jnp.bfloat16)
    zero = jnp.zeros((group_rows, HD), jnp.float32)
    key_new = [
        rotated(kn_ref[t * group_rows : (t + 1) * group_rows, :].astype(jnp.float32), t)
        for t in range(steps)
    ]
    value_new = [
        vn_ref[t * group_rows : (t + 1) * group_rows, :].astype(jnp.float32) for t in range(steps)
    ]
    spare = [zero] * (fresh - steps)
    k_scr[...] = jnp.swapaxes(jnp.stack(key_new + spare, axis=0), 0, 1).astype(jnp.bfloat16)
    v_scr[...] = jnp.swapaxes(jnp.stack(value_new + spare, axis=0), 0, 1).astype(jnp.bfloat16)

    scale = 1.0 / math.sqrt(HD)
    old_slot = lax.broadcasted_iota(jnp.int32, (count, cache_size), 1).astype(jnp.float32)
    new_step = lax.broadcasted_iota(jnp.int32, (count, fresh), 1)
    own_step = lax.broadcasted_iota(jnp.int32, (count, fresh), 0) // heads
    contract = (((1,), (1,)), ((), ()))
    for i in range(slots):
        row = slot_ref[i]
        slab = slabs[i]
        length = row_length(slab[cache_size : cache_size + PAD, :])
        q = q_scr[row]
        old = lax.dot_general(q, slab[:cache_size, :HD], contract, preferred_element_type=jnp.float32)
        new = lax.dot_general(q, k_scr[row], contract, preferred_element_type=jnp.float32)
        old = jnp.where(old_slot < length, old * scale, -1e30)
        new = jnp.where(new_step <= own_step, new * scale, -1e30)
        highest = jnp.maximum(
            jnp.max(old, axis=1, keepdims=True), jnp.max(new, axis=1, keepdims=True)
        )
        old = jnp.exp(old - highest)
        new = jnp.exp(new - highest)
        total = jnp.sum(old, axis=1, keepdims=True) + jnp.sum(new, axis=1, keepdims=True)
        old = (old / total).astype(jnp.bfloat16)
        new = (new / total).astype(jnp.bfloat16)
        o_scr[row] = jnp.dot(
            old, slab[:cache_size, HD:], preferred_element_type=jnp.float32
        ) + jnp.dot(new, v_scr[row], preferred_element_type=jnp.float32)
    for t in range(steps):
        turned = jnp.swapaxes(o_scr[:, t * heads : (t + 1) * heads, :], 0, 1)
        for h in range(heads):
            out_ref[t, :, h * HD : (h + 1) * HD] = turned[h].astype(jnp.bfloat16)


def attend(slot_rows, sums, key_new, value_new, cosine, sine, slabs):
    parts, slots = len(sums), len(slabs)
    steps, group_rows = cosine.shape[:2]
    rows = steps * group_rows
    query_cols = sums[0].shape[1] - key_new.shape[1]
    heads = query_cols // HD
    fresh = 8 * ((steps + 7) // 8)
    whole = lambda *shape: pl.BlockSpec(shape, lambda i: (0,) * len(shape))
    return pl.pallas_call(
        functools.partial(attend_kernel, parts, slots),
        grid=(1,),
        in_specs=[pl.BlockSpec(memory_space=pltpu.SMEM)]
        + [whole(rows, query_cols)] * parts
        + [whole(rows, HD)] * 2
        + [whole(steps, group_rows, HD)] * 2
        + [whole(*slabs[0].shape)] * slots,
        out_specs=whole(steps, group_rows, query_cols),
        out_shape=jax.ShapeDtypeStruct((steps, group_rows, query_cols), jnp.bfloat16),
        scratch_shapes=[
            pltpu.VMEM((group_rows, steps * heads, HD), jnp.bfloat16),
            pltpu.VMEM((group_rows, fresh, HD), jnp.bfloat16),
            pltpu.VMEM((group_rows, fresh, HD), jnp.bfloat16),
            pltpu.VMEM((group_rows, steps * heads, HD), jnp.float32),
        ],
        compiler_params=pltpu.CompilerParams(vmem_limit_bytes=16 * 2**20),
        name="attend",
    )(slot_rows, *sums, key_new, value_new, cosine, sine, *slabs)


def per_device_fast(
    hidden_states,
    query_mantissa,
    query_exponent,
    keyval_mantissa,
    keyval_exponent,
    owner_block,
    cached_kv,
    cache_length,
):
    step_count, group_rows, model_width = hidden_states.shape
    region, block_size, query_cols = query_mantissa.shape
    cache_size = cached_kv.shape[1]
    replicas = lax.axis_size("rep")
    shards = lax.axis_size("tp")
    chips = shards // 2
    rep = lax.axis_index("rep")
    shard = lax.axis_index("tp")
    chip, core = shard // 2, shard % 2
    width = region * block_size
    flat = hidden_states.reshape(step_count * group_rows, model_width)

    def over(axis, size, k):
        return functools.partial(
            lax.ppermute, axis_name=axis, perm=[(i, i ^ k) for i in range(size)]
        )

    features = []
    for k in range(replicas):
        start = owner_block[rep ^ k] * width
        piece = lax.dynamic_slice(flat, (0, start), (flat.shape[0], width))
        features.append(over("rep", replicas, k)(piece) if k else piece)

    cache = cached_kv[0]
    length = cache_length[0]
    digits = jnp.stack([length // DIGIT, length % DIGIT]).astype(jnp.bfloat16)
    tail = jnp.zeros((PAD, 2 * HD), jnp.bfloat16).at[0, :2].set(digits)
    own_slabs = []
    for k in range(chips):
        head = chip ^ k
        keys = lax.dynamic_slice(cache, (0, head * HD), (cache_size, HD))
        values = lax.dynamic_slice(cache, (0, (KVH + head) * HD), (cache_size, HD))
        slab = jnp.concatenate([jnp.concatenate([keys, values], axis=1), tail], axis=0)
        own_slabs.append(over("tp", shards, 2 * k)(slab) if k else slab)
    partner_slabs = [over("tp", shards, 1)(slab) for slab in own_slabs]
    slabs = own_slabs + partner_slabs
    sources = chip ^ jnp.arange(chips, dtype=jnp.int32)
    slot_rows = jnp.concatenate([2 * sources + core, 2 * sources + (1 - core)])

    sums = project(features, query_mantissa, query_exponent, keyval_mantissa, keyval_exponent)
    sums = [over("rep", replicas, k)(part) if k else part for k, part in enumerate(sums)]
    cosine, sine = tables(slot_rows, slabs, step_count, group_rows)

    fresh = sum(part[:, query_cols:].astype(jnp.float32) for part in sums).astype(jnp.bfloat16)
    first = [(s, 2 * s if s < KVH else 2 * (s - KVH) + 1) for s in range(shards)]
    second = [(s, d ^ 1) for s, d in first]
    one = lax.ppermute(fresh, "tp", first)
    two = lax.ppermute(fresh, "tp", second)
    key_new = jnp.where(core == 0, one, two)
    value_new = jnp.where(core == 0, two, one)
    return attend(slot_rows, sums, key_new, value_new, cosine, sine, slabs)


def fast_path_fits(mesh, hidden_states, query_mantissa, keyval_mantissa, cached_kv):
    replicas, shards = mesh.shape["rep"], mesh.shape["tp"]
    rows = hidden_states.shape[1]
    region = query_mantissa.shape[0] // replicas
    return (
        replicas in (2, 4)
        and shards == 2 * KVH
        and query_mantissa.shape[2] == QH * HD
        and keyval_mantissa.shape[2] == 2 * KVH * HD
        and rows == cached_kv.shape[0] == replicas * shards
        and region % CHUNK == 0
        and cached_kv.shape[1] % 128 == 0
        and hidden_states.shape[0] <= 8
    )


def solution(mesh):
    def whole(hidden_states, query_mantissa, query_exponent, keyval_mantissa, *rest):
        fits = fast_path_fits(mesh, hidden_states, query_mantissa, keyval_mantissa, rest[2])
        return jax.shard_map(
            per_device_fast if fits else per_device_general,
            mesh=mesh,
            in_specs=(
                P(None, "rep", None),
                P("rep", None, "tp"),
                P("rep", "tp"),
                P("rep", None, "tp"),
                P("rep", "tp"),
                P(),
                P(("rep", "tp"), None, None),
                P(("rep", "tp")),
            ),
            out_specs=P(None, "rep", "tp"),
            check_vma=False,
        )(hidden_states, query_mantissa, query_exponent, keyval_mantissa, *rest)

    return whole
```

```python
import functools
import math

import jax
import jax.numpy as jnp
from jax import lax
from jax.experimental import pallas as pl
from jax.experimental.pallas import tpu as pltpu
from jax.sharding import PartitionSpec as P

QH = 64
KVH = 4
HD = 128
ROPE_BASE = 500000.0


def dequantize(mantissa, exponent):
    factor = jnp.exp2(exponent.astype(jnp.float32))
    return (mantissa.astype(jnp.float32) * factor[:, None, :]).astype(jnp.bfloat16)


def rotate(vectors, position):
    half_size = vectors.shape[-1] // 2
    frequency = jnp.exp(
        jnp.arange(half_size, dtype=jnp.float32) * (-2.0 * math.log(ROPE_BASE) / vectors.shape[-1])
    )
    angles = position * frequency
    cosine = jnp.cos(angles)
    sine = jnp.sin(angles)
    leading = vectors[..., :half_size]
    trailing = vectors[..., half_size:]
    return jnp.concatenate(
        [leading * cosine - trailing * sine, trailing * cosine + leading * sine], axis=-1
    )


def per_device_general(
    hidden_states,
    query_mantissa,
    query_exponent,
    keyval_mantissa,
    keyval_exponent,
    owner_block,
    cached_kv,
    cache_length,
):
    step_count, group_rows, model_width = hidden_states.shape
    region, block_size, query_cols = query_mantissa.shape
    keyval_cols = keyval_mantissa.shape[2]
    replicas = lax.axis_size("rep")
    flat_rows = step_count * group_rows
    flat = hidden_states.reshape(flat_rows, model_width)
    regions = flat.reshape(flat_rows, replicas, region * block_size)
    outgoing = jnp.take(regions, owner_block, axis=1)
    incoming = lax.all_to_all(outgoing, "rep", split_axis=1, concat_axis=0, tiled=True)
    incoming = incoming.reshape(replicas * flat_rows, region, block_size)
    joined = jnp.concatenate(
        [dequantize(query_mantissa, query_exponent), dequantize(keyval_mantissa, keyval_exponent)],
        axis=2,
    )
    both_sums = lax.psum_scatter(
        jnp.einsum("rbk,bkc->rc", incoming, joined, preferred_element_type=jnp.float32),
        "rep",
        scatter_dimension=0,
        tiled=True,
    )
    query_sum = both_sums[:, :query_cols]
    keyval_sum = both_sums[:, query_cols:]
    query_flat = query_sum.astype(jnp.bfloat16).reshape(step_count, group_rows, query_cols)
    keyval_flat = keyval_sum.astype(jnp.bfloat16).reshape(step_count, group_rows, keyval_cols)
    query_local, keyval_local = (
        lax.all_to_all(query_flat, "tp", split_axis=1, concat_axis=2, tiled=True),
        lax.all_to_all(keyval_flat, "tp", split_axis=1, concat_axis=2, tiled=True),
    )
    local_rows = cache_length.shape[0]
    cache_size = cached_kv.shape[1]
    positions = (
        cache_length.astype(jnp.float32)[None, :]
        + jnp.arange(step_count, dtype=jnp.float32)[:, None]
    )
    query_rot = rotate(
        query_local.reshape(step_count, local_rows, QH, HD).astype(jnp.float32),
        positions[:, :, None, None],
    ).astype(jnp.bfloat16)
    keyval_heads = keyval_local.reshape(step_count, local_rows, 2, KVH, HD)
    key_rot = rotate(keyval_heads[:, :, 0].astype(jnp.float32), positions[:, :, None, None]).astype(
        jnp.bfloat16
    )
    new_values = keyval_heads[:, :, 1]
    old_keys = cached_kv[:, :, : KVH * HD].reshape(local_rows, cache_size, KVH, HD)
    old_values = cached_kv[:, :, KVH * HD :].reshape(local_rows, cache_size, KVH, HD)
    grouped = query_rot.reshape(step_count, local_rows, KVH, QH // KVH, HD)
    score_scale = 1.0 / math.sqrt(HD)
    old_scores = (
        jnp.einsum("trgjd,rcgd->trgjc", grouped, old_keys, preferred_element_type=jnp.float32)
        * score_scale
    )
    new_scores = (
        jnp.einsum("trgjd,srgd->trgjs", grouped, key_rot, preferred_element_type=jnp.float32)
        * score_scale
    )
    old_valid = jnp.arange(cache_size, dtype=jnp.int32)[None, :] < cache_length[:, None]
    new_valid = (
        jnp.arange(step_count, dtype=jnp.int32)[None, :]
        <= jnp.arange(step_count, dtype=jnp.int32)[:, None]
    )
    old_scores = jnp.where(old_valid[None, :, None, None, :], old_scores, -1e30)
    new_scores = jnp.where(new_valid[:, None, None, None, :], new_scores, -1e30)
    highest = jnp.maximum(jnp.max(old_scores, axis=-1), jnp.max(new_scores, axis=-1))[..., None]
    old_exp = jnp.exp(old_scores - highest)
    new_exp = jnp.exp(new_scores - highest)
    denominator = jnp.sum(old_exp, axis=-1, keepdims=True) + jnp.sum(
        new_exp, axis=-1, keepdims=True
    )
    old_weights = (old_exp / denominator).astype(jnp.bfloat16)
    new_weights = (new_exp / denominator).astype(jnp.bfloat16)
    mixed = jnp.einsum(
        "trgjc,rcgd->trgjd", old_weights, old_values, preferred_element_type=jnp.float32
    )
    mixed = mixed + jnp.einsum(
        "trgjs,srgd->trgjd", new_weights, new_values, preferred_element_type=jnp.float32
    )
    outputs = mixed.astype(jnp.bfloat16).reshape(step_count, local_rows, QH * HD)
    return lax.all_to_all(outputs, "tp", split_axis=2, concat_axis=1, tiled=True)


WIRE = jnp.float32
PROJECT_VMEM = 52 * 2**20
PICK_VMEM = 53 * 2**20
CHUNK = 4
PAD = 16
DIGIT = 128


def in_vmem(count):
    return [pl.BlockSpec(memory_space=pltpu.VMEM)] * count


def project_kernel(replicas, *refs):
    slabs = refs[:replicas]
    qm_ref, qf_ref, kvm_ref, kvf_ref = refs[replicas : replicas + 4]
    outs = refs[replicas + 4 : 2 * replicas + 4]
    lhs_ref, qw_ref, kvw_ref, acc_ref, sems = refs[2 * replicas + 4 :]
    rows = slabs[0].shape[0]
    region, block_size, query_cols = qm_ref.shape
    chunks = region // CHUNK
    depth = CHUNK * block_size
    copies = []
    for c in range(chunks):
        part = pl.ds(c * CHUNK, CHUNK)
        copies.append(
            (
                pltpu.make_async_copy(qm_ref.at[part], qw_ref.at[part], sems.at[c, 0]),
                pltpu.make_async_copy(kvm_ref.at[part], kvw_ref.at[part], sems.at[c, 1]),
            )
        )
    for pair in copies:
        for copy in pair:
            copy.start()
    for k in range(replicas):
        lhs_ref[k * rows : (k + 1) * rows, :] = slabs[k][...]

    for c in range(chunks):
        for copy in copies[c]:
            copy.wait()
        lhs = lhs_ref[:, c * depth : (c + 1) * depth]

        def product(w_ref, f_ref):
            blocks = slice(c * CHUNK, (c + 1) * CHUNK)
            weight = w_ref[blocks] * f_ref[blocks, :][:, None, :]
            weight = weight.reshape(depth, weight.shape[2])
            return jnp.dot(lhs, weight, preferred_element_type=jnp.float32)

        query = product(qw_ref, qf_ref)
        keyval = product(kvw_ref, kvf_ref)
        if c == 0:
            acc_ref[:, :query_cols] = query
            acc_ref[:, query_cols:] = keyval
        elif c < chunks - 1:
            acc_ref[:, :query_cols] += query
            acc_ref[:, query_cols:] += keyval
        else:
            for k in range(replicas):
                mine = slice(k * rows, (k + 1) * rows)
                dtype = outs[k].dtype
                outs[k][:, :query_cols] = (acc_ref[mine, :query_cols] + query[mine]).astype(dtype)
                outs[k][:, query_cols:] = (acc_ref[mine, query_cols:] + keyval[mine]).astype(dtype)


def project(slabs, query_mantissa, query_factor, keyval_mantissa, keyval_factor):
    replicas = len(slabs)
    rows, depth = slabs[0].shape
    region, block_size, query_cols = query_mantissa.shape
    cols = query_cols + keyval_mantissa.shape[2]
    weights = pl.BlockSpec(memory_space=pltpu.HBM)
    local = pl.BlockSpec(memory_space=pltpu.VMEM)
    return pl.pallas_call(
        functools.partial(project_kernel, replicas),
        in_specs=[local] * replicas + [weights, local, weights, local],
        out_specs=[local] * replicas,
        out_shape=[
            jax.ShapeDtypeStruct((rows, cols), jnp.float32 if k == 0 else WIRE)
            for k in range(replicas)
        ],
        scratch_shapes=[
            pltpu.VMEM((replicas * rows, depth), jnp.bfloat16),
            pltpu.VMEM(query_mantissa.shape, query_mantissa.dtype),
            pltpu.VMEM(keyval_mantissa.shape, keyval_mantissa.dtype),
            pltpu.VMEM((replicas * rows, cols), jnp.float32),
            pltpu.SemaphoreType.DMA((region // CHUNK, 2)),
        ],
        compiler_params=pltpu.CompilerParams(vmem_limit_bytes=PROJECT_VMEM),
        name="project",
    )(*slabs, query_mantissa, query_factor, keyval_mantissa, keyval_factor)


def pick_features_kernel(replicas, hidden_ref, owner_ref, *refs):
    outs, sems = refs[:replicas], refs[replicas]
    rep = lax.axis_index("rep")
    width = outs[0].shape[2]
    copies = []
    for k in range(replicas):
        start = pl.multiple_of(owner_ref[rep ^ k] * width, width)
        copies.append(
            pltpu.make_async_copy(hidden_ref.at[:, :, pl.ds(start, width)], outs[k], sems.at[k])
        )
    for copy in copies:
        copy.start()
    for copy in copies:
        copy.wait()


def pick_features(hidden_states, owner_block, replicas, width):
    shape = hidden_states.shape[:2] + (width,)
    return pl.pallas_call(
        functools.partial(pick_features_kernel, replicas),
        in_specs=[
            pl.BlockSpec(memory_space=pltpu.HBM),
            pl.BlockSpec(memory_space=pltpu.SMEM),
        ],
        out_specs=[pl.BlockSpec(memory_space=pltpu.VMEM)] * replicas,
        out_shape=[jax.ShapeDtypeStruct(shape, hidden_states.dtype)] * replicas,
        scratch_shapes=[pltpu.SemaphoreType.DMA((replicas,))],
        compiler_params=pltpu.CompilerParams(vmem_limit_bytes=PICK_VMEM),
        name="pick_features",
    )(hidden_states, owner_block)


def pick_slabs_kernel(chips, cache_ref, length_ref, qe_ref, kve_ref, *refs):
    outs, qf_ref, kvf_ref, sems = refs[:chips], refs[chips], refs[chips + 1], refs[chips + 2]
    chip = lax.axis_index("tp") // 2
    size = cache_ref.shape[1]
    copies = []
    for k in range(chips):
        head = chip ^ k
        for side in range(2):
            start = pl.multiple_of((side * chips + head) * HD, HD)
            copies.append(
                pltpu.make_async_copy(
                    cache_ref.at[0, :, pl.ds(start, HD)],
                    outs[k].at[pl.ds(0, size), pl.ds(side * HD, HD)],
                    sems.at[k, side],
                )
            )
    for copy in copies:
        copy.start()
    length = length_ref[0]
    lane = lax.broadcasted_iota(jnp.int32, (PAD, 2 * HD), 1)
    tail = jnp.where(lane == 0, length // DIGIT, length % DIGIT).astype(jnp.float32)
    for k in range(chips):
        outs[k][size:, :] = tail.astype(jnp.bfloat16)
    for e_ref, f_ref in ((qe_ref, qf_ref), (kve_ref, kvf_ref)):
        f_ref[...] = jnp.exp2(e_ref[...].astype(jnp.float32)).astype(jnp.bfloat16)
    for copy in copies:
        copy.wait()


def pick_slabs(cached_kv, cache_length, query_exponent, keyval_exponent, chips):
    shape = (cached_kv.shape[1] + PAD, 2 * HD)
    return pl.pallas_call(
        functools.partial(pick_slabs_kernel, chips),
        in_specs=[
            pl.BlockSpec(memory_space=pltpu.HBM),
            pl.BlockSpec(memory_space=pltpu.SMEM),
        ]
        + in_vmem(2),
        out_specs=in_vmem(chips + 2),
        out_shape=[jax.ShapeDtypeStruct(shape, cached_kv.dtype)] * chips
        + [
            jax.ShapeDtypeStruct(query_exponent.shape, jnp.bfloat16),
            jax.ShapeDtypeStruct(keyval_exponent.shape, jnp.bfloat16),
        ],
        scratch_shapes=[pltpu.SemaphoreType.DMA((chips, 2))],
        compiler_params=pltpu.CompilerParams(vmem_limit_bytes=8 * 2**20),
        name="pick_slabs",
    )(cached_kv, cache_length, query_exponent, keyval_exponent)


def slab_row(i, chips):
    shard = lax.axis_index("tp")
    source = (shard // 2) ^ (i % chips)
    core = shard % 2
    return 2 * source + (core if i < chips else 1 - core)


def row_length(slab_ref):
    tail = slab_ref[slab_ref.shape[0] - PAD :, :].astype(jnp.float32)
    return tail[0:1, 0:1] * DIGIT + tail[0:1, 1:2]


def tables_kernel(slots, *refs):
    slabs = refs[:slots]
    cos_ref, sin_ref = refs[slots:]
    steps, group_rows, width = cos_ref.shape
    half = width // 2
    row = lax.broadcasted_iota(jnp.int32, (group_rows, width), 0)
    lane = lax.broadcasted_iota(jnp.int32, (group_rows, width), 1)
    length = jnp.zeros((group_rows, width), jnp.float32)
    for i in range(slots):
        length = jnp.where(row == slab_row(i, slots // 2), row_length(slabs[i]), length)
    index = jnp.where(lane < half, lane, lane - half).astype(jnp.float32)
    frequency = jnp.exp(index * (-2.0 * math.log(ROPE_BASE) / width))
    for t in range(steps):
        angles = (length + float(t)) * frequency
        cos_ref[t] = jnp.cos(angles)
        sine = jnp.sin(angles)
        sin_ref[t] = jnp.where(lane < half, -sine, sine)


def tables(slabs, steps, group_rows):
    shape = (steps, group_rows, HD)
    return pl.pallas_call(
        functools.partial(tables_kernel, len(slabs)),
        in_specs=in_vmem(len(slabs)),
        out_specs=in_vmem(2),
        out_shape=[jax.ShapeDtypeStruct(shape, jnp.float32)] * 2,
        compiler_params=pltpu.CompilerParams(vmem_limit_bytes=8 * 2**20),
        name="tables",
    )(*slabs)


def rotated(x, cosine, sine):
    return x * cosine + pltpu.roll(x, x.shape[-1] // 2, 1) * sine


CONTRACT_LAST = (((1,), (1,)), ((), ()))
SCALE = 1.0 / math.sqrt(HD)


def score_kernel(parts, slots, *refs):
    sums = refs[:parts]
    cos_ref, sin_ref = refs[parts : parts + 2]
    slabs = refs[parts + 2 : parts + 2 + slots]
    q_ref, score_ref = refs[parts + 2 + slots :]
    steps, group_rows, _ = cos_ref.shape
    heads = q_ref.shape[1] // steps
    cache_size = score_ref.shape[2]
    for t in range(steps):
        rows = slice(t * group_rows, (t + 1) * group_rows)
        by_head = []
        for h in range(heads):
            cols = slice(h * HD, (h + 1) * HD)
            x = sums[0][rows, cols]
            for part in sums[1:]:
                x = x + part[rows, cols].astype(jnp.float32)
            x = x.astype(jnp.bfloat16).astype(jnp.float32)
            by_head.append(rotated(x, cos_ref[t], sin_ref[t]))
        turned = jnp.swapaxes(jnp.stack(by_head, axis=0), 0, 1)
        q_ref[:, t * heads : (t + 1) * heads, :] = turned.astype(jnp.bfloat16)
    count = steps * heads
    slot = lax.broadcasted_iota(jnp.int32, (count, cache_size), 1).astype(jnp.float32)
    for i in range(slots):
        q = q_ref[slab_row(i, slots // 2)]
        score = lax.dot_general(
            q, slabs[i][:cache_size, :HD], CONTRACT_LAST, preferred_element_type=jnp.float32
        )
        score_ref[i] = jnp.where(slot < row_length(slabs[i]), score * SCALE, -1e30)


def scores(sums, cosine, sine, slabs, query_cols):
    parts, slots = len(sums), len(slabs)
    steps, group_rows = cosine.shape[:2]
    count = steps * (query_cols // HD)
    return pl.pallas_call(
        functools.partial(score_kernel, parts, slots),
        in_specs=in_vmem(parts + 2 + slots),
        out_specs=in_vmem(2),
        out_shape=[
            jax.ShapeDtypeStruct((group_rows, count, HD), jnp.bfloat16),
            jax.ShapeDtypeStruct((slots, count, slabs[0].shape[0] - PAD), jnp.float32),
        ],
        compiler_params=pltpu.CompilerParams(vmem_limit_bytes=16 * 2**20),
        name="scores",
    )(*sums, cosine, sine, *slabs)


def attend_kernel(slots, one_ref, two_ref, cos_ref, sin_ref, q_ref, score_ref, *refs):
    slabs = refs[:slots]
    out_ref, k_scr, v_scr, o_scr = refs[slots:]
    steps, group_rows, query_cols = out_ref.shape
    heads = query_cols // HD
    fresh = k_scr.shape[1]
    count = steps * heads
    cache_size = score_ref.shape[2]
    first = lax.axis_index("tp") % 2 == 0
    one = one_ref[...].astype(jnp.float32)
    two = two_ref[...].astype(jnp.float32)
    keys = jnp.where(first, one, two)
    values = jnp.where(first, two, one)
    spare = [jnp.zeros((group_rows, HD), jnp.float32)] * (fresh - steps)
    of_step = lambda x, t: x[t * group_rows : (t + 1) * group_rows]
    key_new = [rotated(of_step(keys, t), cos_ref[t], sin_ref[t]) for t in range(steps)]
    value_new = [of_step(values, t) for t in range(steps)]
    k_scr[...] = jnp.swapaxes(jnp.stack(key_new + spare, axis=0), 0, 1).astype(jnp.bfloat16)
    v_scr[...] = jnp.swapaxes(jnp.stack(value_new + spare, axis=0), 0, 1).astype(jnp.bfloat16)
    new_step = lax.broadcasted_iota(jnp.int32, (count, fresh), 1)
    own_step = lax.broadcasted_iota(jnp.int32, (count, fresh), 0) // heads
    for i in range(slots):
        row = slab_row(i, slots // 2)
        old = score_ref[i]
        new = lax.dot_general(
            q_ref[row], k_scr[row], CONTRACT_LAST, preferred_element_type=jnp.float32
        )
        new = jnp.where(new_step <= own_step, new * SCALE, -1e30)
        highest = jnp.maximum(
            jnp.max(old, axis=1, keepdims=True), jnp.max(new, axis=1, keepdims=True)
        )
        old = jnp.exp(old - highest)
        new = jnp.exp(new - highest)
        total = jnp.sum(old, axis=1, keepdims=True) + jnp.sum(new, axis=1, keepdims=True)
        old = (old / total).astype(jnp.bfloat16)
        new = (new / total).astype(jnp.bfloat16)
        o_scr[row] = jnp.dot(
            old, slabs[i][:cache_size, HD:], preferred_element_type=jnp.float32
        ) + jnp.dot(new, v_scr[row], preferred_element_type=jnp.float32)
    for t in range(steps):
        turned = jnp.swapaxes(o_scr[:, t * heads : (t + 1) * heads, :], 0, 1)
        for h in range(heads):
            out_ref[t, :, h * HD : (h + 1) * HD] = turned[h].astype(jnp.bfloat16)


def attend(one, two, cosine, sine, queries, score, slabs):
    slots = len(slabs)
    steps, group_rows = cosine.shape[:2]
    count = queries.shape[1]
    query_cols = count // steps * HD
    fresh = 8 * ((steps + 7) // 8)
    return pl.pallas_call(
        functools.partial(attend_kernel, slots),
        in_specs=in_vmem(6 + slots),
        out_specs=pl.BlockSpec(memory_space=pltpu.VMEM),
        out_shape=jax.ShapeDtypeStruct((steps, group_rows, query_cols), jnp.bfloat16),
        scratch_shapes=[
            pltpu.VMEM((group_rows, fresh, HD), jnp.bfloat16),
            pltpu.VMEM((group_rows, fresh, HD), jnp.bfloat16),
            pltpu.VMEM((group_rows, count, HD), jnp.float32),
        ],
        compiler_params=pltpu.CompilerParams(vmem_limit_bytes=16 * 2**20),
        name="attend",
    )(one, two, cosine, sine, queries, score, *slabs)


def per_device_fast(
    hidden_states,
    query_mantissa,
    query_exponent,
    keyval_mantissa,
    keyval_exponent,
    owner_block,
    cached_kv,
    cache_length,
):
    step_count, group_rows, model_width = hidden_states.shape
    region, block_size, query_cols = query_mantissa.shape
    replicas = lax.axis_size("rep")
    shards = lax.axis_size("tp")
    chips = shards // 2
    width = region * block_size

    def over(axis, size, k):
        return functools.partial(
            lax.ppermute, axis_name=axis, perm=[(i, i ^ k) for i in range(size)]
        )

    features = pick_features(hidden_states, owner_block, replicas, width)
    features = [x.reshape(step_count * group_rows, width) for x in features]
    features = [over("rep", replicas, k)(x) if k else x for k, x in enumerate(features)]

    *slabs, query_factor, keyval_factor = pick_slabs(
        cached_kv, cache_length, query_exponent, keyval_exponent, chips
    )
    slabs = [over("tp", shards, 2 * k)(x) if k else x for k, x in enumerate(slabs)]
    slabs = slabs + [over("tp", shards, 1)(x) for x in slabs]

    sums = project(features, query_mantissa, query_factor, keyval_mantissa, keyval_factor)
    sums = [over("rep", replicas, k)(part) if k else part for k, part in enumerate(sums)]
    cosine, sine = tables(slabs, step_count, group_rows)

    fresh = sum(part[:, query_cols:].astype(jnp.float32) for part in sums).astype(jnp.bfloat16)
    first = [(s, 2 * s if s < KVH else 2 * (s - KVH) + 1) for s in range(shards)]
    one = lax.ppermute(fresh, "tp", first)
    two = lax.ppermute(fresh, "tp", [(s, d ^ 1) for s, d in first])
    queries, score = scores(sums, cosine, sine, slabs, query_cols)
    return attend(one, two, cosine, sine, queries, score, slabs)


def fast_path_fits(mesh, hidden_states, query_mantissa, keyval_mantissa, cached_kv):
    replicas, shards = mesh.shape["rep"], mesh.shape["tp"]
    rows = hidden_states.shape[1]
    region = query_mantissa.shape[0] // replicas
    return (
        replicas in (2, 4)
        and shards == 2 * KVH
        and query_mantissa.shape[2] == QH * HD
        and keyval_mantissa.shape[2] == 2 * KVH * HD
        and rows == cached_kv.shape[0] == replicas * shards
        and region % CHUNK == 0
        and cached_kv.shape[1] % 128 == 0
        and hidden_states.shape[0] <= 8
    )


def solution(mesh):
    def whole(hidden_states, query_mantissa, query_exponent, keyval_mantissa, *rest):
        fits = fast_path_fits(mesh, hidden_states, query_mantissa, keyval_mantissa, rest[2])
        return jax.shard_map(
            per_device_fast if fits else per_device_general,
            mesh=mesh,
            in_specs=(
                P(None, "rep", None),
                P("rep", None, "tp"),
                P("rep", "tp"),
                P("rep", None, "tp"),
                P("rep", "tp"),
                P(),
                P(("rep", "tp"), None, None),
                P(("rep", "tp")),
            ),
            out_specs=P(None, "rep", "tp"),
            check_vma=False,
        )(hidden_states, query_mantissa, query_exponent, keyval_mantissa, *rest)

    return whole
```
